32 devices in a mesh: dp: 8 (over z, x), latent: 4 (over y, core).
Axes of the slice: x: 2, y: 2, z: 4, core: 2. Of those that a mesh axis runs over, the one named last changes fastest.
Arguments:
- tokens: bfloat16 [1024, 1536], P('dp'), may hold values from -6 to 6
- enc_weight: bfloat16 [1536, 32768], P(None, ('dp', 'latent')), may hold values from -0.15625 to 0.15625
- enc_bias: float32 [32768], P(('dp', 'latent')), may hold values from -3 to 3
- dec_weight: bfloat16 [32768, 1536], P(('dp', 'latent')), may hold values from -0.0625 to 0.0625
- dec_bias: float32 [1536], replicated, may hold values from -3 to 3
- slot_token: int32 [1024], P(('dp', 'latent')), may hold values from 0 to 7
- slot_latent: int32 [1024], P(('dp', 'latent')), may hold values from 0 to 7
- slot_count: int32 [32], P(('dp', 'latent')), may hold values from 6 to 32, as said below
Outputs:
- enc_grad: bfloat16 [1536, 32768], P(None, ('dp', 'latent'))
- dec_grad: bfloat16 [32768, 1536], P(('dp', 'latent'))
- enc_bias_grad: float32 [32768], P(('dp', 'latent'))
- dec_bias_grad: float32 [1536], replicated
- mean_error: float32 [], replicated
The draws below stay inside these ranges and needn't reach their ends.
Inputs may be any that keep to these rules, and one draw needn't show every extreme that they name: `slot_count`: slot lists of one device never repeat a (token block, latent block) pair among its 32 slots; entries past a device's count name valid blocks and are ignored; some device has all 32 slots live in every draw.
All inputs are finite; a program needn't handle non-finite values.
Results may differ from the reference program's by a relative error of at most 0.0065.
Values may be sent and summed in bfloat16 or wider, within the bound.
A program may use at most 128 MiB of HBM per device.

```python
import jax
import jax.numpy as jnp
from jax import lax

D = 1536
LAT_DEV = 1024
BLK = 128
CAP = 32
LB_DEV = 8
OWNERS = 32
LATENTS = 32768
TOKENS = 1024
TBLOCKS = 8


def slot_tables(key):
    base = jax.random.fold_in(key, 7)
    key_score, key_count, key_hot = jax.random.split(base, 3)
    combos = TBLOCKS * LB_DEV
    scores = jax.random.randint(key_score, (OWNERS, combos), 0, 2 ** 20, dtype=jnp.int32) * combos + jnp.arange(combos, dtype=jnp.int32)[None, :]
    picks = lax.top_k(scores, CAP)[1].astype(jnp.int32)
    divisor = jax.random.randint(key_count, (OWNERS,), 1, 6, dtype=jnp.int32)
    counts = jnp.maximum(CAP // divisor, 1)
    hottest = jax.random.randint(key_hot, (), 0, OWNERS, dtype=jnp.int32)
    counts = jnp.where(jnp.arange(OWNERS, dtype=jnp.int32) == hottest, CAP, counts).astype(jnp.int32)
    return (picks // LB_DEV, picks % LB_DEV, counts)


def draw_slot_token(key, part):
    return slot_tables(key)[0].reshape(-1).astype(jnp.int32)


def draw_slot_latent(key, part):
    return slot_tables(key)[1].reshape(-1).astype(jnp.int32)


def draw_slot_count(key, part):
    return slot_tables(key)[2].astype(jnp.int32)


def block_levels(own_key, dims, pieces, low, high):
    def one(position, shards_of):
        steps = jax.random.uniform(jax.random.fold_in(jax.random.fold_in(own_key, 6), position), (shards_of,), jnp.float32, low / len(pieces), high / len(pieces))
        return jnp.repeat(jnp.exp(steps), dims[position] // shards_of).reshape((-1,) + (1,) * (len(dims) - position - 1))

    gain = one(*pieces[0])
    for cut in pieces[1:]:
        gain = gain * one(*cut)
    return gain


def bell_draw(rng, shape, width, limit, pieces=(), kind=jnp.bfloat16):
    result = jax.random.normal(rng, shape, jnp.float32) * width
    if len(pieces) > 0:
        result = block_levels(rng, shape, pieces, -0.22, 0.18) * result
    return jnp.clip(result, min=-limit, max=limit).astype(kind)


def setup_inputs(seed: int = 0) -> dict:
    keys = jax.random.split(jax.random.key(seed), 9)
    tokens = bell_draw(keys[0], (TOKENS, D), 1.0, 6.0, ((0, 8),))
    enc_weight = bell_draw(keys[1], (D, LATENTS), D ** -0.5, 0.15625, ((1, 32),))
    enc_bias = bell_draw(keys[2], (LATENTS,), 0.5, 3.0, ((0, 32),), jnp.float32)
    dec_weight = bell_draw(keys[3], (LATENTS, D), (OWNERS * CAP * BLK // (2 * TBLOCKS)) ** -0.5, 0.0625, ((0, 32),))
    dec_bias = bell_draw(keys[4], (D,), 0.5, 3.0, (), jnp.float32)
    slot_token = draw_slot_token(jax.random.fold_in(keys[8], 71), 0)
    slot_latent = draw_slot_latent(jax.random.fold_in(keys[8], 71), 0)
    slot_count = draw_slot_count(jax.random.fold_in(keys[8], 71), 0)
    return {"tokens": tokens, "enc_weight": enc_weight, "enc_bias": enc_bias, "dec_weight": dec_weight, "dec_bias": dec_bias, "slot_token": slot_token, "slot_latent": slot_latent, "slot_count": slot_count}


def reference(tokens, enc_weight, enc_bias, dec_weight, dec_bias, slot_token, slot_latent, slot_count):
    token_table = slot_token.reshape(OWNERS, CAP)
    latent_table = slot_latent.reshape(OWNERS, CAP)

    def forward_owner(partial_value, owner):
        base = owner * LAT_DEV
        enc_local = lax.dynamic_slice_in_dim(enc_weight, base, LAT_DEV, 1)
        bias_local = lax.dynamic_slice_in_dim(enc_bias, base, LAT_DEV, 0)
        dec_local = lax.dynamic_slice_in_dim(dec_weight, base, LAT_DEV, 0)
        token_row = token_table[owner]
        latent_row = latent_table[owner]

        def one_slot(slot_index, carried):
            activations, partial_value = carried
            row_start = (token_row[slot_index] * BLK).astype(jnp.int32)
            col_start = (latent_row[slot_index] * BLK).astype(jnp.int32)
            tok_rows = lax.dynamic_slice_in_dim(tokens, row_start, BLK, 0)
            enc_block = lax.dynamic_slice_in_dim(enc_local, col_start, BLK, 1)
            bias_block = lax.dynamic_slice_in_dim(bias_local, col_start, BLK, 0)
            active = (jnp.dot(tok_rows, enc_block, preferred_element_type=jnp.float32) + bias_block[None, :]).astype(jnp.bfloat16)
            dec_block = lax.dynamic_slice_in_dim(dec_local, col_start, BLK, 0)
            contrib = jnp.dot(active, dec_block, preferred_element_type=jnp.float32)
            previous = lax.dynamic_slice_in_dim(partial_value, row_start, BLK, 0)
            partial_value = lax.dynamic_update_slice_in_dim(partial_value, previous + contrib, row_start, 0)
            activations = lax.dynamic_update_index_in_dim(activations, active, slot_index, 0)
            return activations, partial_value

        empty = jnp.zeros((CAP, BLK, BLK), jnp.bfloat16)
        activations, partial_value = lax.fori_loop(0, slot_count[owner], one_slot, (empty, partial_value))
        return partial_value, activations

    start_sum = jnp.zeros((TOKENS, D), jnp.float32)
    recon, all_acts = lax.scan(forward_owner, start_sum, jnp.arange(OWNERS, dtype=jnp.int32))
    residual = recon + dec_bias[None, :] - tokens.astype(jnp.float32)
    mean_error = jnp.sum(residual * residual) / (TOKENS * D)
    scaled = residual * 0.25
    dec_bias_grad = jnp.sum(scaled, axis=0)
    grad_rows = scaled.astype(jnp.bfloat16)

    def backward_owner(inputs):
        owner, activations = inputs
        base = owner * LAT_DEV
        dec_local = lax.dynamic_slice_in_dim(dec_weight, base, LAT_DEV, 0)
        token_row = token_table[owner]
        latent_row = latent_table[owner]

        def one_slot(slot_index, gradients):
            enc_acc, dec_acc, bias_acc = gradients
            row_start = (token_row[slot_index] * BLK).astype(jnp.int32)
            col_start = (latent_row[slot_index] * BLK).astype(jnp.int32)
            tok_rows = lax.dynamic_slice_in_dim(tokens, row_start, BLK, 0)
            grad_block = lax.dynamic_slice_in_dim(grad_rows, row_start, BLK, 0)
            dec_block = lax.dynamic_slice_in_dim(dec_local, col_start, BLK, 0)
            pre_grad = lax.dot_general(grad_block, dec_block, (((1,), (1,)), ((), ())), preferred_element_type=jnp.float32)
            old_bias = lax.dynamic_slice_in_dim(bias_acc, col_start, BLK, 0)
            bias_acc = lax.dynamic_update_slice_in_dim(bias_acc, old_bias + jnp.sum(pre_grad, axis=0), col_start, 0)
            pre_half = pre_grad.astype(jnp.bfloat16)
            enc_term = lax.dot_general(tok_rows, pre_half, (((0,), (0,)), ((), ())), preferred_element_type=jnp.float32)
            old_enc = lax.dynamic_slice_in_dim(enc_acc, col_start, BLK, 1)
            enc_acc = lax.dynamic_update_slice_in_dim(enc_acc, old_enc + enc_term, col_start, 1)
            dec_term = lax.dot_general(activations[slot_index], grad_block, (((0,), (0,)), ((), ())), preferred_element_type=jnp.float32)
            old_dec = lax.dynamic_slice_in_dim(dec_acc, col_start, BLK, 0)
            dec_acc = lax.dynamic_update_slice_in_dim(dec_acc, old_dec + dec_term, col_start, 0)
            return enc_acc, dec_acc, bias_acc

        start_grads = (jnp.zeros((D, LAT_DEV), jnp.float32), jnp.zeros((LAT_DEV, D), jnp.float32), jnp.zeros((LAT_DEV,), jnp.float32))
        enc_acc, dec_acc, bias_acc = lax.fori_loop(0, slot_count[owner], one_slot, start_grads)
        return enc_acc.astype(jnp.bfloat16), dec_acc.astype(jnp.bfloat16), bias_acc

    enc_stack, dec_stack, bias_stack = lax.map(backward_owner, (jnp.arange(OWNERS, dtype=jnp.int32), all_acts))
    enc_grad = jnp.transpose(enc_stack, (1, 0, 2)).reshape(D, OWNERS * LAT_DEV)
    dec_grad = dec_stack.reshape(OWNERS * LAT_DEV, D)
    enc_bias_grad = bias_stack.reshape(OWNERS * LAT_DEV)
    return enc_grad, dec_grad, enc_bias_grad, dec_bias_grad, mean_error
```

```python
import functools

import jax
import jax.numpy as jnp
from jax import lax
from jax.experimental import pallas as pl
from jax.experimental.pallas import tpu as pltpu
from jax.sharding import PartitionSpec as P

BLK = 128
MESH = pl.DeviceIdType.MESH
F32 = jnp.float32
BF16 = jnp.bfloat16
DMA = pltpu.SemaphoreType.DMA


def loop(low, high, body):
    def step(k, carry):
        body(k)
        return carry

    lax.fori_loop(low, high, step, jnp.int32(0))


class Place:
    def __init__(self, depth, width):
        self.depth, self.width = depth, width
        self.dp, self.lat = lax.axis_index("dp"), lax.axis_index("latent")
        self.z, self.x = self.dp // 2, self.dp % 2
        self.y, self.c = self.lat // 2, self.lat % 2
        self.ox, self.oc = 1 - self.x, 1 - self.c

    def zat(self, k):
        return (self.z + k) % self.depth

    def yat(self, j):
        return (self.y + j) % self.width

    def to_z(self, zz):
        return (zz * 2 + self.x, self.lat)

    def to_x(self):
        return (self.z * 2 + self.ox, self.lat)

    def to_y(self, yy):
        return (self.dp, yy * 2 + self.c)

    def to_c(self):
        return (self.dp, self.y * 2 + self.oc)

    def barrier(self):
        sem = pltpu.get_barrier_semaphore()
        peers = [self.to_z(self.zat(k)) for k in range(1, self.depth)]
        peers += [self.to_x()]
        peers += [self.to_y(self.yat(j)) for j in range(1, self.width)]
        peers += [self.to_c()]
        for peer in peers:
            pl.semaphore_signal(sem, inc=1, device_id=peer, device_id_type=MESH)
        pl.semaphore_wait(sem, len(peers))


def remote(src, dst, send, recv, peer):
    return pltpu.make_async_remote_copy(
        src_ref=src, dst_ref=dst, send_sem=send, recv_sem=recv, device_id=peer, device_id_type=MESH
    )


def gather_sems(depth, width):
    dps = depth * 2
    return [
        DMA((2, dps, width)),
        DMA((2, dps)),
        DMA((2, depth)),
        DMA((depth,)),
        DMA((dps, width)),
        DMA((depth, width)),
        DMA((depth, width)),
        DMA((2, dps)),
    ]


def gather(at, buf, sems):
    got, got_c, s_z, s_ax, s_ay, s_by, s_bx, s_c = sems
    depth, width = at.depth, at.width
    half = buf.shape[-1] // 2
    cols = (pl.ds(0, half), pl.ds(half, half))

    def shard(d, yy, h):
        return buf.at[d, yy, at.c, :, cols[h]]

    def copy(d, yy, h, send, peer):
        return remote(shard(d, yy, h), shard(d, yy, h), send, got.at[h, d, yy], peer)

    def core(d, h, cc):
        ref = buf.at[d, :, cc, :, cols[h]]
        return remote(ref, ref, s_c.at[h, d], got_c.at[h, d], at.to_c())

    def arrive(d, yy, h):
        copy(d, yy, h, s_z.at[h, 0], at.to_x()).wait_recv()

    def z_copy(k, h):
        return copy(at.dp, at.y, h, s_z.at[h, k], at.to_z(at.zat(k)))

    def ax(k):
        return copy(at.zat(k) * 2 + at.x, at.y, 0, s_ax.at[k], at.to_x())

    def ay(k, other, j):
        d = at.zat(k) * 2 + (at.ox if other else at.x)
        return copy(d, at.y, 0, s_ay.at[k * 2 + other, j], at.to_y(at.yat(j)))

    def by(k, j):
        return copy(at.zat(k) * 2 + at.x, at.y, 1, s_by.at[k, j], at.to_y(at.yat(j)))

    def bx(k, j):
        return copy(at.zat(k) * 2 + at.x, at.yat(j), 1, s_bx.at[k, j], at.to_x())

    def first(k):
        ax(k).start()
        for j in range(1, width):
            by(k, j).start()
        for j in range(1, width):
            ay(k, 0, j).start()
        bx(k, 0).start()

    for k in range(1, depth):
        for h in range(2):
            z_copy(k, h).start()
    first(0)

    def relay(k):
        for h in range(2):
            arrive(at.zat(k) * 2 + at.x, at.y, h)
        first(k)

    loop(1, depth, relay)

    def cross(k):
        d, od = at.zat(k) * 2 + at.x, at.zat(k) * 2 + at.ox
        arrive(od, at.y, 0)
        for j in range(1, width):
            ay(k, 1, j).start()
        for j in range(1, width):
            arrive(d, at.yat(j), 1)
            bx(k, j).start()
        core(d, 1, at.c).start()

    loop(0, depth, cross)

    def last(k):
        d, od = at.zat(k) * 2 + at.x, at.zat(k) * 2 + at.ox
        for dd in (d, od):
            for j in range(1, width):
                arrive(dd, at.yat(j), 0)
            core(dd, 0, at.c).start()
        for j in range(width):
            arrive(od, at.yat(j), 1)
        core(od, 1, at.c).start()

    loop(0, depth, last)

    def settle(k):
        d, od = at.zat(k) * 2 + at.x, at.zat(k) * 2 + at.ox
        for dd in (d, od):
            for h in range(2):
                core(dd, h, at.oc).wait_recv()
                core(dd, h, at.c).wait_send()
        ax(k).wait_send()
        bx(k, 0).wait_send()
        for j in range(1, width):
            ay(k, 0, j).wait_send()
            ay(k, 1, j).wait_send()
            by(k, j).wait_send()
            bx(k, j).wait_send()

    loop(0, depth, settle)
    for k in range(1, depth):
        for h in range(2):
            z_copy(k, h).wait_send()


def token_kernel(depth, width, tok_ref, buf, *sems):
    at = Place(depth, width)
    at.barrier()
    buf[at.dp, at.y, at.c] = tok_ref[at.y, at.c]
    gather(at, buf, sems)


def gather_tokens(tokens, depth, width):
    feats = tokens.shape[1]
    rows = tokens.shape[0] // (width * 2)
    vmem = pl.BlockSpec(memory_space=pltpu.VMEM)
    out = pl.pallas_call(
        functools.partial(token_kernel, depth, width),
        out_shape=jax.ShapeDtypeStruct((depth * 2, width, 2, rows, feats), BF16),
        in_specs=[vmem],
        out_specs=vmem,
        scratch_shapes=gather_sems(depth, width),
        compiler_params=pltpu.CompilerParams(
            collective_id=0, has_side_effects=True, vmem_limit_bytes=32 * 2 ** 20
        ),
        name="gather_tokens",
    )(tokens.reshape(width, 2, rows, feats))
    return out.reshape(-1, feats)


def reduce_kernel(depth, width, part, tok_ref, bias_ref, buf, stat_ref, *scratch):
    rc, a1, rya, a2a, rxa, rxb, a2b, ryb, a3, rz, tz, tx, ty, tc = scratch[:14]
    (s_c, g_c, s_ya, g_ya, s_xb, g_xb, s_xa, g_xa, s_yb, g_yb, s_z, g_z) = scratch[14:26]
    (s_tz, g_tz, s_tx, g_tx, s_ty, g_ty, s_tc, g_tc) = scratch[26:34]
    sems = scratch[34:]
    at = Place(depth, width)
    half = part.shape[-1] // 2
    low, high = pl.ds(0, half), pl.ds(half, half)
    at.barrier()

    def c_copy(d):
        return remote(part.at[d, :, at.oc], rc.at[d], s_c.at[d], g_c.at[d], at.to_c())

    def ya(d, j):
        yy = at.yat(j)
        return remote(a1.at[d, yy, :, low], rya.at[at.y, d], s_ya.at[d, j], g_ya.at[at.y, d], at.to_y(yy))

    def ya_in(d, yy):
        return remote(rya.at[yy, d], rya.at[yy, d], s_ya.at[d, 0], g_ya.at[yy, d], at.to_x())

    def xb(zz):
        return remote(a1.at[zz * 2 + at.ox, :, :, high], rxb.at[zz], s_xb.at[zz], g_xb.at[zz], at.to_x())

    def xa(zz):
        return remote(a2a.at[zz * 2 + at.ox], rxa.at[zz], s_xa.at[zz], g_xa.at[zz], at.to_x())

    def yb(zz, j):
        yy = at.yat(j)
        return remote(a2b.at[zz, yy], ryb.at[at.y, zz], s_yb.at[zz, j], g_yb.at[at.y, zz], at.to_y(yy))

    def yb_in(zz, yy):
        return remote(ryb.at[yy, zz], ryb.at[yy, zz], s_yb.at[zz, 0], g_yb.at[yy, zz], at.to_x())

    def zc(k):
        zz = at.zat(k)
        return remote(a3.at[zz], rz.at[at.z], s_z.at[k], g_z.at[at.z], at.to_z(zz))

    def z_in(zz):
        return remote(rz.at[zz], rz.at[zz], s_z.at[0], g_z.at[zz], at.to_x())

    def each(k):
        return at.zat(k + 1)

    def begin(k):
        c_copy(each(k) * 2 + at.ox).start()
        c_copy(each(k) * 2 + at.x).start()

    loop(0, depth, begin)

    def one(k):
        zz = each(k)
        for xx in (at.ox, at.x):
            d = zz * 2 + xx
            c_copy(d).wait_recv()
            a1[d] = (part[d, :, at.c].astype(F32) + rc[d].astype(F32)).astype(BF16)
            if xx is at.ox:
                xb(zz).start()
            for j in range(1, width):
                ya(d, j).start()

    loop(0, depth, one)

    def two(k):
        zz = each(k)
        for xx in (at.ox, at.x):
            d = zz * 2 + xx
            total = a1[d, at.y, :, low].astype(F32)
            for j in range(1, width):
                ya_in(d, at.yat(j)).wait_recv()
                total = total + rya[at.yat(j), d].astype(F32)
            a2a[d] = total.astype(BF16)
            if xx is at.ox:
                xa(zz).start()
        xb(zz).wait_recv()
        a2b[zz] = (a1[zz * 2 + at.x, :, :, high].astype(F32) + rxb[zz].astype(F32)).astype(BF16)
        for j in range(1, width):
            yb(zz, j).start()

    loop(0, depth, two)

    def sum_a(zz):
        xa(zz).wait_recv()
        return a2a[zz * 2 + at.x].astype(F32) + rxa[zz].astype(F32)

    def sum_b(zz):
        total = a2b[zz, at.y].astype(F32)
        for j in range(1, width):
            yb_in(zz, at.yat(j)).wait_recv()
            total = total + ryb[at.yat(j), zz].astype(F32)
        return total

    def three(k):
        zz = at.zat(k)
        a3[zz, :, low] = sum_a(zz).astype(BF16)
        a3[zz, :, high] = sum_b(zz).astype(BF16)
        zc(k).start()

    loop(1, depth, three)
    own = jnp.concatenate([sum_a(at.z), sum_b(at.z)], axis=-1)
    for k in range(1, depth):
        zz = at.zat(k)
        z_in(zz).wait_recv()
        own = own + rz[zz].astype(F32)
    residual = own + bias_ref[...] - tok_ref[at.y, at.c].astype(F32)
    scaled = residual * 0.25
    buf[at.dp, at.y, at.c] = scaled.astype(BF16)
    tz[at.z, 0:1, :] = jnp.sum(scaled, axis=0, keepdims=True)
    tz[at.z, 1:2, :] = jnp.sum(residual * residual, axis=0, keepdims=True)

    def tz_copy(k):
        return remote(tz.at[at.z], tz.at[at.z], s_tz.at[k], g_tz.at[at.z], at.to_z(at.zat(k)))

    def tz_in(zz):
        return remote(tz.at[zz], tz.at[zz], s_tz.at[0], g_tz.at[zz], at.to_x())

    for k in range(1, depth):
        tz_copy(k).start()
    gather(at, buf, sems)
    for k in range(1, depth):
        tz_in(at.zat(k)).wait_recv()
    tx[at.x] = jnp.sum(tz[...], axis=0)
    x_stat = remote(tx.at[at.x], tx.at[at.x], s_tx, g_tx, at.to_x())
    x_stat.start()
    x_stat.wait_recv()
    ty[at.y] = tx[0] + tx[1]

    def ty_copy(j):
        return remote(ty.at[at.y], ty.at[at.y], s_ty.at[j], g_ty.at[at.y], at.to_y(at.yat(j)))

    for j in range(1, width):
        ty_copy(j).start()
    for j in range(1, width):
        yy = at.yat(j)
        remote(ty.at[yy], ty.at[yy], s_ty.at[0], g_ty.at[yy], at.to_x()).wait_recv()
    tc[at.c] = jnp.sum(ty[...], axis=0)
    c_stat = remote(tc.at[at.c], tc.at[at.c], s_tc, g_tc, at.to_c())
    c_stat.start()
    c_stat.wait_recv()
    stat_ref[...] = tc[0] + tc[1]

    x_stat.wait_send()
    c_stat.wait_send()
    for j in range(1, width):
        ty_copy(j).wait_send()
    for k in range(1, depth):
        tz_copy(k).wait_send()
        zc(k).wait_send()

    def settle(k):
        zz = each(k)
        for xx in (at.ox, at.x):
            d = zz * 2 + xx
            c_copy(d).wait_send()
            for j in range(1, width):
                ya(d, j).wait_send()
        xb(zz).wait_send()
        xa(zz).wait_send()
        for j in range(1, width):
            yb(zz, j).wait_send()

    loop(0, depth, settle)


def reduce_gather(partial_value, tokens, dec_bias, depth, width):
    feats = tokens.shape[1]
    rows = tokens.shape[0] // (width * 2)
    dps, half = depth * 2, feats // 2
    vmem = pl.BlockSpec(memory_space=pltpu.VMEM)
    block = pltpu.VMEM
    scratch = [
        block((dps, width, rows, feats), BF16),
        block((dps, width, rows, feats), BF16),
        block((width, dps, rows, half), BF16),
        block((dps, rows, half), BF16),
        block((depth, rows, half), BF16),
        block((depth, width, rows, half), BF16),
        block((depth, width, rows, half), BF16),
        block((width, depth, rows, half), BF16),
        block((depth, rows, feats), BF16),
        block((depth, rows, feats), BF16),
        block((depth, 2, feats), F32),
        block((2, 2, feats), F32),
        block((width, 2, feats), F32),
        block((2, 2, feats), F32),
        DMA((dps,)), DMA((dps,)),
        DMA((dps, width)), DMA((width, dps)),
        DMA((depth,)), DMA((depth,)),
        DMA((depth,)), DMA((depth,)),
        DMA((depth, width)), DMA((width, depth)),
        DMA((depth,)), DMA((depth,)),
        DMA((depth,)), DMA((depth,)),
        DMA, DMA,
        DMA((width,)), DMA((width,)),
        DMA, DMA,
    ] + gather_sems(depth, width)
    grads, stats = pl.pallas_call(
        functools.partial(reduce_kernel, depth, width),
        out_shape=(
            jax.ShapeDtypeStruct((dps, width, 2, rows, feats), BF16),
            jax.ShapeDtypeStruct((2, feats), F32),
        ),
        in_specs=[vmem] * 3,
        out_specs=(vmem, vmem),
        scratch_shapes=scratch,
        compiler_params=pltpu.CompilerParams(
            collective_id=1, has_side_effects=True, vmem_limit_bytes=48 * 2 ** 20
        ),
        name="reduce_gather",
    )(
        partial_value.reshape(dps, width, 2, rows, feats),
        tokens.reshape(width, 2, rows, feats),
        dec_bias.reshape(1, feats),
    )
    return grads.reshape(-1, feats), stats


def local(depth, width, tokens, enc_weight, enc_bias, dec_weight, dec_bias, slot_token, slot_latent, slot_count):
    feats = tokens.shape[1]
    latents = enc_weight.shape[1]
    total_rows = tokens.shape[0] * depth * 2
    t_blocks, l_blocks = total_rows // BLK, latents // BLK
    alive = jnp.arange(slot_token.shape[0], dtype=jnp.int32) < slot_count[0]
    at_token = (slot_token[:, None] == jnp.arange(t_blocks, dtype=jnp.int32)[None, :]) & alive[:, None]
    at_latent = slot_latent[:, None] == jnp.arange(l_blocks, dtype=jnp.int32)[None, :]
    live = jnp.any(at_token[:, :, None] & at_latent[:, None, :], axis=0)
    mask = jnp.broadcast_to(live[:, None, :, None], (t_blocks, BLK, l_blocks, BLK)).reshape(total_rows, latents)

    gathered = gather_tokens(tokens, depth, width)
    dense = jnp.dot(gathered, enc_weight, preferred_element_type=F32) + enc_bias[None, :]
    active = jnp.where(mask, dense, 0.0).astype(BF16)
    partial_value = jnp.dot(active, dec_weight, preferred_element_type=F32).astype(BF16)
    grads, stats = reduce_gather(partial_value, tokens, dec_bias, depth, width)
    pre = lax.dot_general(grads, dec_weight, (((1,), (1,)), ((), ())), preferred_element_type=F32)
    pre = jnp.where(mask, pre, 0.0)
    bias_grad = jnp.sum(pre, axis=0)
    enc_grad = lax.dot_general(
        gathered, pre.astype(BF16), (((0,), (0,)), ((), ())), preferred_element_type=F32
    ).astype(BF16)
    dec_grad = lax.dot_general(active, grads, (((0,), (0,)), ((), ())), preferred_element_type=F32).astype(BF16)
    return enc_grad, dec_grad, bias_grad, stats[0], jnp.sum(stats[1]) / (total_rows * feats)


def solution(mesh):
    depth, width = mesh.shape["dp"] // 2, mesh.shape["latent"] // 2
    in_specs = (
        P("dp", None),
        P(None, ("dp", "latent")),
        P(("dp", "latent")),
        P(("dp", "latent"), None),
        P(),
        P(("dp", "latent")),
        P(("dp", "latent")),
        P(("dp", "latent")),
    )
    out_specs = (
        P(None, ("dp", "latent")),
        P(("dp", "latent"), None),
        P(("dp", "latent")),
        P(),
        P(),
    )
    return jax.shard_map(
        functools.partial(local, depth, width), mesh=mesh, in_specs=in_specs, out_specs=out_specs, check_vma=False
    )
```

```python
import functools

import jax
import jax.numpy as jnp
from jax import lax
from jax.experimental import pallas as pl
from jax.experimental.pallas import tpu as pltpu
from jax.sharding import PartitionSpec as P

BLK = 128
MESH = pl.DeviceIdType.MESH
F32 = jnp.float32
BF16 = jnp.bfloat16
DMA = pltpu.SemaphoreType.DMA


def loop(low, high, body):
    def step(k, carry):
        body(k)
        return carry

    lax.fori_loop(low, high, step, jnp.int32(0))


class Place:
    def __init__(self, depth, width):
        self.depth, self.width = depth, width
        self.dp, self.lat = lax.axis_index("dp"), lax.axis_index("latent")
        self.z, self.x = self.dp // 2, self.dp % 2
        self.y, self.c = self.lat // 2, self.lat % 2
        self.ox, self.oc = 1 - self.x, 1 - self.c

    def zat(self, k):
        return (self.z + k) % self.depth

    def yat(self, j):
        return (self.y + j) % self.width

    def to_z(self, zz):
        return (zz * 2 + self.x, self.lat)

    def to_x(self):
        return (self.z * 2 + self.ox, self.lat)

    def to_y(self, yy):
        return (self.dp, yy * 2 + self.c)

    def to_c(self):
        return (self.dp, self.y * 2 + self.oc)

    def barrier(self):
        sem = pltpu.get_barrier_semaphore()
        peers = [self.to_z(self.zat(k)) for k in range(1, self.depth)]
        peers += [self.to_x()]
        peers += [self.to_y(self.yat(j)) for j in range(1, self.width)]
        peers += [self.to_c()]
        for peer in peers:
            pl.semaphore_signal(sem, inc=1, device_id=peer, device_id_type=MESH)
        pl.semaphore_wait(sem, len(peers))


def remote(src, dst, send, recv, peer):
    return pltpu.make_async_remote_copy(
        src_ref=src, dst_ref=dst, send_sem=send, recv_sem=recv, device_id=peer, device_id_type=MESH
    )


def gather_sems(depth, width):
    dps = depth * 2
    return [
        DMA((2, dps, width)),
        DMA((2, dps, width)),
        DMA((2, depth)),
        DMA((depth,)),
        DMA((dps, width)),
        DMA((depth, width)),
        DMA((depth, width)),
        DMA((2, dps, width)),
    ]


def gather(at, buf, sems, hooks=()):
    got, got_c, s_z, s_ax, s_ay, s_by, s_bx, s_c = sems
    depth, width = at.depth, at.width
    half = buf.shape[-1] // 2
    cols = (pl.ds(0, half), pl.ds(half, half))

    def shard(d, yy, h):
        return buf.at[d, yy, at.c, :, cols[h]]

    def copy(d, yy, h, send, peer):
        return remote(shard(d, yy, h), shard(d, yy, h), send, got.at[h, d, yy], peer)

    def core(d, yy, h, cc):
        ref = buf.at[d, yy, cc, :, cols[h]]
        return remote(ref, ref, s_c.at[h, d, yy], got_c.at[h, d, yy], at.to_c())

    def arrive(d, yy, h):
        copy(d, yy, h, s_z.at[h, 0], at.to_x()).wait_recv()

    def z_copy(k, h):
        return copy(at.dp, at.y, h, s_z.at[h, k], at.to_z(at.zat(k)))

    def near(k):
        return at.zat(k) * 2 + at.x

    def far(k):
        return at.zat(k) * 2 + at.ox

    def ax(k):
        return copy(near(k), at.y, 0, s_ax.at[k], at.to_x())

    def ay(k, other, j):
        return copy(far(k) if other else near(k), at.y, 0, s_ay.at[k * 2 + other, j], at.to_y(at.yat(j)))

    def by(k, j):
        return copy(near(k), at.y, 1, s_by.at[k, j], at.to_y(at.yat(j)))

    def bx(k, j):
        return copy(near(k), at.yat(j), 1, s_bx.at[k, j], at.to_x())

    def first(k):
        ax(k).start()
        for j in range(1, width):
            by(k, j).start()
        for j in range(1, width):
            ay(k, 0, j).start()
        bx(k, 0).start()
        for h in range(2):
            core(near(k), at.y, h, at.c).start()

    def cross(k):
        arrive(far(k), at.y, 0)
        for j in range(1, width):
            ay(k, 1, j).start()
        core(far(k), at.y, 0, at.c).start()
        for j in range(1, width):
            arrive(near(k), at.yat(j), 1)
            bx(k, j).start()
            core(near(k), at.yat(j), 1, at.c).start()

    def last(k):
        for dd in (near(k), far(k)):
            for j in range(1, width):
                arrive(dd, at.yat(j), 0)
                core(dd, at.yat(j), 0, at.c).start()
        for j in range(width):
            arrive(far(k), at.yat(j), 1)
            core(far(k), at.yat(j), 1, at.c).start()

    for k in range(1, depth):
        for h in range(2):
            z_copy(k, h).start()
    first(0)

    def relay(k):
        for h in range(2):
            arrive(near(k), at.y, h)
        first(k)
        cross(k - 1)

    loop(1, depth, relay)
    for hook in hooks[:1]:
        hook()
    cross(depth - 1)
    for hook in hooks[1:2]:
        hook()
    loop(0, depth, last)
    for hook in hooks[2:3]:
        hook()

    def settle(k):
        for dd in (near(k), far(k)):
            for j in range(width):
                for h in range(2):
                    core(dd, at.yat(j), h, at.oc).wait_recv()
                    core(dd, at.yat(j), h, at.c).wait_send()
        ax(k).wait_send()
        bx(k, 0).wait_send()
        for j in range(1, width):
            ay(k, 0, j).wait_send()
            ay(k, 1, j).wait_send()
            by(k, j).wait_send()
            bx(k, j).wait_send()

    loop(0, depth, settle)
    for k in range(1, depth):
        for h in range(2):
            z_copy(k, h).wait_send()


def token_kernel(depth, width, tok_ref, buf, *sems):
    at = Place(depth, width)
    at.barrier()
    buf[at.dp, at.y, at.c] = tok_ref[at.y, at.c]
    gather(at, buf, sems)


def gather_tokens(tokens, depth, width):
    feats = tokens.shape[1]
    rows = tokens.shape[0] // (width * 2)
    whole = depth * 2 * tokens.size * 2
    vmem = pl.BlockSpec(memory_space=pltpu.VMEM)
    out = pl.pallas_call(
        functools.partial(token_kernel, depth, width),
        out_shape=jax.ShapeDtypeStruct((depth * 2, width, 2, rows, feats), BF16),
        in_specs=[vmem],
        out_specs=vmem,
        scratch_shapes=gather_sems(depth, width),
        compiler_params=pltpu.CompilerParams(
            collective_id=0, has_side_effects=True, vmem_limit_bytes=3 * whole + 2 ** 21
        ),
        name="gather_tokens",
    )(tokens.reshape(width, 2, rows, feats))
    return out.reshape(-1, feats)


def reduce_kernel(depth, width, part, tok_ref, bias_ref, buf, stat_ref, *scratch):
    rc, a1, rya, a2a, rxa, rxb, a2b, ryb, a3, rz, tz, tx, ty, tc = scratch[:14]
    (s_c, g_c, s_ya, g_ya, s_xb, g_xb, s_xa, g_xa, s_yb, g_yb, s_z, g_z) = scratch[14:26]
    (s_tz, g_tz, s_tx, g_tx, s_ty, g_ty, s_tc, g_tc) = scratch[26:34]
    sems = scratch[34:]
    at = Place(depth, width)
    half = part.shape[-1] // 2
    low, high = pl.ds(0, half), pl.ds(half, half)
    at.barrier()

    def c_copy(d):
        return remote(part.at[d, :, at.oc], rc.at[d], s_c.at[d], g_c.at[d], at.to_c())

    def ya(d, j):
        yy = at.yat(j)
        return remote(a1.at[d, yy, :, low], rya.at[at.y, d], s_ya.at[d, j], g_ya.at[at.y, d], at.to_y(yy))

    def ya_in(d, yy):
        return remote(rya.at[yy, d], rya.at[yy, d], s_ya.at[d, 0], g_ya.at[yy, d], at.to_x())

    def xb(zz):
        return remote(a1.at[zz * 2 + at.ox, :, :, high], rxb.at[zz], s_xb.at[zz], g_xb.at[zz], at.to_x())

    def xa(zz):
        return remote(a2a.at[zz * 2 + at.ox], rxa.at[zz], s_xa.at[zz], g_xa.at[zz], at.to_x())

    def yb(zz, j):
        yy = at.yat(j)
        return remote(a2b.at[zz, yy], ryb.at[at.y, zz], s_yb.at[zz, j], g_yb.at[at.y, zz], at.to_y(yy))

    def yb_in(zz, yy):
        return remote(ryb.at[yy, zz], ryb.at[yy, zz], s_yb.at[zz, 0], g_yb.at[yy, zz], at.to_x())

    def zc(k):
        zz = at.zat(k)
        return remote(a3.at[zz], rz.at[at.z], s_z.at[k], g_z.at[at.z], at.to_z(zz))

    def z_in(zz):
        return remote(rz.at[zz], rz.at[zz], s_z.at[0], g_z.at[zz], at.to_x())

    def each(k):
        return at.zat(k + 1)

    def begin(k):
        c_copy(each(k) * 2 + at.ox).start()
        c_copy(each(k) * 2 + at.x).start()

    loop(0, depth, begin)

    def one(k):
        zz = each(k)
        for xx in (at.ox, at.x):
            d = zz * 2 + xx
            c_copy(d).wait_recv()
            a1[d] = (part[d, :, at.c].astype(F32) + rc[d].astype(F32)).astype(BF16)
            if xx is at.ox:
                xb(zz).start()
            for j in range(1, width):
                ya(d, j).start()

    def two(k):
        zz = each(k)
        for xx in (at.ox, at.x):
            d = zz * 2 + xx
            total = a1[d, at.y, :, low].astype(F32)
            for j in range(1, width):
                ya_in(d, at.yat(j)).wait_recv()
                total = total + rya[at.yat(j), d].astype(F32)
            a2a[d] = total.astype(BF16)
            if xx is at.ox:
                xa(zz).start()
        xb(zz).wait_recv()
        a2b[zz] = (a1[zz * 2 + at.x, :, :, high].astype(F32) + rxb[zz].astype(F32)).astype(BF16)
        for j in range(1, width):
            yb(zz, j).start()

    def sum_a(zz):
        xa(zz).wait_recv()
        return a2a[zz * 2 + at.x].astype(F32) + rxa[zz].astype(F32)

    def sum_b(zz):
        total = a2b[zz, at.y].astype(F32)
        for j in range(1, width):
            yb_in(zz, at.yat(j)).wait_recv()
            total = total + ryb[at.yat(j), zz].astype(F32)
        return total

    def three(k):
        zz = each(k)
        a3[zz, :, low] = sum_a(zz).astype(BF16)
        a3[zz, :, high] = sum_b(zz).astype(BF16)
        zc(k + 1).start()

    one(0)
    one(1)
    two(0)

    def pipeline(k):
        one(k)
        two(k - 1)
        three(k - 2)

    loop(2, depth, pipeline)
    two(depth - 1)
    three(depth - 2)
    own = jnp.concatenate([sum_a(at.z), sum_b(at.z)], axis=-1)
    for k in range(1, depth):
        zz = at.zat(k)
        z_in(zz).wait_recv()
        own = own + rz[zz].astype(F32)
    residual = own + bias_ref[...] - tok_ref[at.y, at.c].astype(F32)
    scaled = residual * 0.25
    buf[at.dp, at.y, at.c] = scaled.astype(BF16)
    tz[at.z, 0:1, :] = jnp.sum(scaled, axis=0, keepdims=True)
    tz[at.z, 1:2, :] = jnp.sum(residual * residual, axis=0, keepdims=True)

    def tz_copy(k):
        return remote(tz.at[at.z], tz.at[at.z], s_tz.at[k], g_tz.at[at.z], at.to_z(at.zat(k)))

    def tz_in(zz):
        return remote(tz.at[zz], tz.at[zz], s_tz.at[0], g_tz.at[zz], at.to_x())

    for k in range(1, depth):
        tz_copy(k).start()
    x_stat = remote(tx.at[at.x], tx.at[at.x], s_tx, g_tx, at.to_x())
    c_stat = remote(tc.at[at.c], tc.at[at.c], s_tc, g_tc, at.to_c())

    def ty_copy(j):
        return remote(ty.at[at.y], ty.at[at.y], s_ty.at[j], g_ty.at[at.y], at.to_y(at.yat(j)))

    def stat_x():
        for k in range(1, depth):
            tz_in(at.zat(k)).wait_recv()
        tx[at.x] = jnp.sum(tz[...], axis=0)
        x_stat.start()

    def stat_y():
        x_stat.wait_recv()
        ty[at.y] = tx[0] + tx[1]
        for j in range(1, width):
            ty_copy(j).start()

    def stat_c():
        for j in range(1, width):
            yy = at.yat(j)
            remote(ty.at[yy], ty.at[yy], s_ty.at[0], g_ty.at[yy], at.to_x()).wait_recv()
        tc[at.c] = jnp.sum(ty[...], axis=0)
        c_stat.start()

    gather(at, buf, sems, (stat_x, stat_y, stat_c))
    c_stat.wait_recv()
    stat_ref[...] = tc[0] + tc[1]

    x_stat.wait_send()
    c_stat.wait_send()
    for j in range(1, width):
        ty_copy(j).wait_send()
    for k in range(1, depth):
        tz_copy(k).wait_send()
        zc(k).wait_send()

    def settle(k):
        zz = each(k)
        for xx in (at.ox, at.x):
            d = zz * 2 + xx
            c_copy(d).wait_send()
            for j in range(1, width):
                ya(d, j).wait_send()
        xb(zz).wait_send()
        xa(zz).wait_send()
        for j in range(1, width):
            yb(zz, j).wait_send()

    loop(0, depth, settle)


def reduce_gather(partial_value, tokens, dec_bias, depth, width):
    feats = tokens.shape[1]
    rows = tokens.shape[0] // (width * 2)
    dps, half = depth * 2, feats // 2
    whole = partial_value.size * 2
    vmem = pl.BlockSpec(memory_space=pltpu.VMEM)
    block = pltpu.VMEM
    scratch = [
        block((dps, width, rows, feats), BF16),
        block((dps, width, rows, feats), BF16),
        block((width, dps, rows, half), BF16),
        block((dps, rows, half), BF16),
        block((depth, rows, half), BF16),
        block((depth, width, rows, half), BF16),
        block((depth, width, rows, half), BF16),
        block((width, depth, rows, half), BF16),
        block((depth, rows, feats), BF16),
        block((depth, rows, feats), BF16),
        block((depth, 2, feats), F32),
        block((2, 2, feats), F32),
        block((width, 2, feats), F32),
        block((2, 2, feats), F32),
        DMA((dps,)), DMA((dps,)),
        DMA((dps, width)), DMA((width, dps)),
        DMA((depth,)), DMA((depth,)),
        DMA((depth,)), DMA((depth,)),
        DMA((depth, width)), DMA((width, depth)),
        DMA((depth,)), DMA((depth,)),
        DMA((depth,)), DMA((depth,)),
        DMA, DMA,
        DMA((width,)), DMA((width,)),
        DMA, DMA,
    ] + gather_sems(depth, width)
    grads, stats = pl.pallas_call(
        functools.partial(reduce_kernel, depth, width),
        out_shape=(
            jax.ShapeDtypeStruct((dps, width, 2, rows, feats), BF16),
            jax.ShapeDtypeStruct((2, feats), F32),
        ),
        in_specs=[vmem] * 3,
        out_specs=(vmem, vmem),
        scratch_shapes=scratch,
        compiler_params=pltpu.CompilerParams(
            collective_id=1, has_side_effects=True, vmem_limit_bytes=5 * whole + 2 ** 21
        ),
        name="reduce_gather",
    )(
        partial_value.reshape(dps, width, 2, rows, feats),
        tokens.reshape(width, 2, rows, feats),
        dec_bias.reshape(1, feats),
    )
    return grads.reshape(-1, feats), stats


def backward_kernel(tok_ref, act_ref, grad_ref, dec_ref, live_ref, enc_out, dec_out, bias_out, flipped):
    @pl.when(pl.program_id(0) == 0)
    def _():
        flipped[...] = tok_ref[...].T

    pre = lax.dot_general(grad_ref[...], dec_ref[...], (((1,), (1,)), ((), ())), preferred_element_type=F32)
    pieces = [
        jnp.where(live_ref[t : t + 1, :] > 0, pre[t * BLK : (t + 1) * BLK], 0.0) for t in range(live_ref.shape[0])
    ]
    pre = jnp.concatenate(pieces, axis=0)
    bias_out[...] = jnp.sum(pre, axis=0, keepdims=True)
    enc_out[...] = jnp.dot(flipped[...], pre.astype(BF16), preferred_element_type=F32).astype(BF16)
    dec_out[...] = lax.dot_general(
        act_ref[...], grad_ref[...], (((0,), (0,)), ((), ())), preferred_element_type=F32
    ).astype(BF16)


def backward(gathered, active, grads, dec_weight, live):
    rows, feats = gathered.shape
    latents = dec_weight.shape[0]
    tile = 2 * BLK
    live_cols = jnp.repeat(live.astype(F32), BLK, axis=1)
    vmem = pl.BlockSpec(memory_space=pltpu.VMEM)
    return pl.pallas_call(
        backward_kernel,
        grid=(latents // tile,),
        out_shape=(
            jax.ShapeDtypeStruct((feats, latents), BF16),
            jax.ShapeDtypeStruct((latents, feats), BF16),
            jax.ShapeDtypeStruct((1, latents), F32),
        ),
        in_specs=[
            vmem,
            pl.BlockSpec((rows, tile), lambda i: (0, i)),
            vmem,
            pl.BlockSpec((tile, feats), lambda i: (i, 0)),
            pl.BlockSpec((live.shape[0], tile), lambda i: (0, i)),
        ],
        out_specs=(
            pl.BlockSpec((feats, tile), lambda i: (0, i)),
            pl.BlockSpec((tile, feats), lambda i: (i, 0)),
            pl.BlockSpec((1, tile), lambda i: (0, i)),
        ),
        scratch_shapes=[pltpu.VMEM((feats, rows), BF16)],
        compiler_params=pltpu.CompilerParams(vmem_limit_bytes=10 * rows * feats),
        name="backward",
    )(gathered, active, grads, dec_weight, live_cols)


def local(depth, width, tokens, enc_weight, enc_bias, dec_weight, dec_bias, slot_token, slot_latent, slot_count):
    feats = tokens.shape[1]
    latents = enc_weight.shape[1]
    total_rows = tokens.shape[0] * depth * 2
    t_blocks, l_blocks = total_rows // BLK, latents // BLK
    alive = jnp.arange(slot_token.shape[0], dtype=jnp.int32) < slot_count[0]
    at_token = (slot_token[:, None] == jnp.arange(t_blocks, dtype=jnp.int32)[None, :]) & alive[:, None]
    at_latent = slot_latent[:, None] == jnp.arange(l_blocks, dtype=jnp.int32)[None, :]
    live = jnp.any(at_token[:, :, None] & at_latent[:, None, :], axis=0)
    mask = jnp.broadcast_to(live[:, None, :, None], (t_blocks, BLK, l_blocks, BLK)).reshape(total_rows, latents)

    gathered = gather_tokens(tokens, depth, width)
    dense = jnp.dot(gathered, enc_weight, preferred_element_type=F32) + enc_bias[None, :]
    active = jnp.where(mask, dense, 0.0).astype(BF16)
    partial_value = jnp.dot(active, dec_weight, preferred_element_type=F32).astype(BF16)
    grads, stats = reduce_gather(partial_value, tokens, dec_bias, depth, width)
    enc_grad, dec_grad, bias_grad = backward(gathered, active, grads, dec_weight, live)
    return enc_grad, dec_grad, bias_grad.reshape(latents), stats[0], jnp.sum(stats[1]) / (total_rows * feats)


def solution(mesh):
    depth, width = mesh.shape["dp"] // 2, mesh.shape["latent"] // 2
    in_specs = (
        P("dp", None),
        P(None, ("dp", "latent")),
        P(("dp", "latent")),
        P(("dp", "latent"), None),
        P(),
        P(("dp", "latent")),
        P(("dp", "latent")),
        P(("dp", "latent")),
    )
    out_specs = (
        P(None, ("dp", "latent")),
        P(("dp", "latent"), None),
        P(("dp", "latent")),
        P(),
        P(),
    )
    return jax.shard_map(
        functools.partial(local, depth, width), mesh=mesh, in_specs=in_specs, out_specs=out_specs, check_vma=False
    )
```

```python
import functools

import jax
import jax.numpy as jnp
from jax import lax
from jax.experimental import pallas as pl
from jax.experimental.pallas import tpu as pltpu
from jax.sharding import PartitionSpec as P

BLK = 128
MESH = pl.DeviceIdType.MESH
F32 = jnp.float32
BF16 = jnp.bfloat16
DMA = pltpu.SemaphoreType.DMA


def loop(low, high, body):
    def step(k, carry):
        body(k)
        return carry

    lax.fori_loop(low, high, step, jnp.int32(0))


class Place:
    def __init__(self, depth, width):
        self.depth, self.width = depth, width
        self.dp, self.lat = lax.axis_index("dp"), lax.axis_index("latent")
        self.z, self.x = self.dp // 2, self.dp % 2
        self.y, self.c = self.lat // 2, self.lat % 2
        self.ox, self.oc = 1 - self.x, 1 - self.c

    def zat(self, k):
        return (self.z + k) % self.depth

    def yat(self, j):
        return (self.y + j) % self.width

    def to_z(self, zz):
        return (zz * 2 + self.x, self.lat)

    def to_x(self):
        return (self.z * 2 + self.ox, self.lat)

    def to_y(self, yy):
        return (self.dp, yy * 2 + self.c)

    def to_c(self):
        return (self.dp, self.y * 2 + self.oc)

    def barrier(self):
        sem = pltpu.get_barrier_semaphore()
        peers = [self.to_z(self.zat(k)) for k in range(1, self.depth)]
        peers += [self.to_x()]
        peers += [self.to_y(self.yat(j)) for j in range(1, self.width)]
        peers += [self.to_c()]
        for peer in peers:
            pl.semaphore_signal(sem, inc=1, device_id=peer, device_id_type=MESH)
        pl.semaphore_wait(sem, len(peers))


def remote(src, dst, send, recv, peer):
    return pltpu.make_async_remote_copy(
        src_ref=src, dst_ref=dst, send_sem=send, recv_sem=recv, device_id=peer, device_id_type=MESH
    )


def gather_sems(depth, width):
    dps = depth * 2
    return [
        DMA((2, dps, width)),
        DMA((2, dps, width)),
        DMA((2, depth)),
        DMA((depth,)),
        DMA((dps, width)),
        DMA((depth, width)),
        DMA((depth, width)),
        DMA((2, dps, width)),
    ]


def gather(at, buf, sems, hooks=(), held=False):
    got, got_c, s_z, s_ax, s_ay, s_by, s_bx, s_c = sems
    depth, width = at.depth, at.width
    half = buf.shape[-1] // 2
    cols = (pl.ds(0, half), pl.ds(half, half))

    def shard(d, yy, h):
        return buf.at[d, yy, at.c, :, cols[h]]

    def copy(d, yy, h, send, peer):
        return remote(shard(d, yy, h), shard(d, yy, h), send, got.at[h, d, yy], peer)

    def core(d, yy, h, cc):
        ref = buf.at[d, yy, cc, :, cols[h]]
        return remote(ref, ref, s_c.at[h, d, yy], got_c.at[h, d, yy], at.to_c())

    def arrive(d, yy, h):
        copy(d, yy, h, s_z.at[h, 0], at.to_x()).wait_recv()

    def z_copy(k, h):
        return copy(at.dp, at.y, h, s_z.at[h, k], at.to_z(at.zat(k)))

    def near(k):
        return at.zat(k) * 2 + at.x

    def far(k):
        return at.zat(k) * 2 + at.ox

    def ax(k):
        return copy(near(k), at.y, 0, s_ax.at[k], at.to_x())

    def ay(k, other, j):
        return copy(far(k) if other else near(k), at.y, 0, s_ay.at[k * 2 + other, j], at.to_y(at.yat(j)))

    def by(k, j):
        return copy(near(k), at.y, 1, s_by.at[k, j], at.to_y(at.yat(j)))

    def bx(k, j):
        return copy(near(k), at.yat(j), 1, s_bx.at[k, j], at.to_x())

    def mine(k):
        return held and isinstance(k, int) and k == 0

    def first(k):
        ax(k).start()
        if not mine(k):
            for j in range(1, width):
                by(k, j).start()
            for j in range(1, width):
                ay(k, 0, j).start()
        bx(k, 0).start()
        if mine(k):
            for j in range(1, width):
                bx(k, j).start()
            return
        for h in range(2):
            core(near(k), at.y, h, at.c).start()

    def cross(k):
        arrive(far(k), at.y, 0)
        for j in range(1, width):
            ay(k, 1, j).start()
        core(far(k), at.y, 0, at.c).start()
        if mine(k):
            return
        for j in range(1, width):
            arrive(near(k), at.yat(j), 1)
            bx(k, j).start()
            core(near(k), at.yat(j), 1, at.c).start()

    def last(k):
        for dd in (far(k),) if mine(k) else (near(k), far(k)):
            for j in range(1, width):
                arrive(dd, at.yat(j), 0)
                core(dd, at.yat(j), 0, at.c).start()
        for j in range(width):
            arrive(far(k), at.yat(j), 1)
            core(far(k), at.yat(j), 1, at.c).start()

    for k in range(1, depth):
        for h in range(2):
            z_copy(k, h).start()
    first(0)

    def relay(k):
        for h in range(2):
            arrive(near(k), at.y, h)
        first(k)

    relay(1)
    cross(0)

    def both(k):
        relay(k)
        cross(k - 1)

    loop(2, depth, both)
    for hook in hooks[:1]:
        hook()
    cross(depth - 1)
    for hook in hooks[1:2]:
        hook()
    last(0)
    loop(1, depth, last)
    for hook in hooks[2:3]:
        hook()

    def settle(k):
        for dd in (far(k),) if mine(k) else (near(k), far(k)):
            for j in range(width):
                for h in range(2):
                    core(dd, at.yat(j), h, at.oc).wait_recv()
                    core(dd, at.yat(j), h, at.c).wait_send()
        ax(k).wait_send()
        bx(k, 0).wait_send()
        for j in range(1, width):
            if not mine(k):
                ay(k, 0, j).wait_send()
                by(k, j).wait_send()
            ay(k, 1, j).wait_send()
            bx(k, j).wait_send()

    settle(0)
    loop(1, depth, settle)
    for k in range(1, depth):
        for h in range(2):
            z_copy(k, h).wait_send()


def token_kernel(depth, width, tok_ref, buf, load_sem, *sems):
    at = Place(depth, width)
    load = pltpu.make_async_copy(tok_ref, buf.at[at.dp], load_sem)
    load.start()
    at.barrier()
    load.wait()
    gather(at, buf, sems, held=True)


def gather_tokens(tokens, depth, width):
    feats = tokens.shape[1]
    rows = tokens.shape[0] // (width * 2)
    whole = depth * 2 * tokens.size * 2
    vmem = pl.BlockSpec(memory_space=pltpu.VMEM)
    out = pl.pallas_call(
        functools.partial(token_kernel, depth, width),
        out_shape=jax.ShapeDtypeStruct((depth * 2, width, 2, rows, feats), BF16),
        in_specs=[pl.BlockSpec(memory_space=pl.ANY)],
        out_specs=vmem,
        scratch_shapes=[DMA] + gather_sems(depth, width),
        compiler_params=pltpu.CompilerParams(
            collective_id=0, has_side_effects=True, vmem_limit_bytes=3 * whole + 2 ** 21
        ),
        name="gather_tokens",
    )(tokens.reshape(width, 2, rows, feats))
    return out.reshape(-1, feats)


def reduce_kernel(depth, width, act_ref, dec_ref, tok_ref, bias_ref, buf, stat_ref, part, *scratch):
    rc, a1, rya, a2a, rxa, rxb, a2b, ryb, a3, rz, tz, tx, ty, tc = scratch[:14]
    (s_c, g_c, s_ya, g_ya, s_xb, g_xb, s_xa, g_xa, s_yb, g_yb, s_z, g_z) = scratch[14:26]
    (s_tz, g_tz, s_tx, g_tx, s_ty, g_ty, s_tc, g_tc) = scratch[26:34]
    sems = scratch[34:]
    at = Place(depth, width)
    half = buf.shape[-1] // 2
    low, high = pl.ds(0, half), pl.ds(half, half)
    at.barrier()

    def c_copy(d):
        return remote(part.at[d, :, at.oc], rc.at[d], s_c.at[d], g_c.at[d], at.to_c())

    def ya(d, j):
        yy = at.yat(j)
        return remote(a1.at[d, yy, :, low], rya.at[at.y, d], s_ya.at[d, j], g_ya.at[at.y, d], at.to_y(yy))

    def ya_in(d, yy):
        return remote(rya.at[yy, d], rya.at[yy, d], s_ya.at[d, 0], g_ya.at[yy, d], at.to_x())

    def xb(zz):
        return remote(a1.at[zz * 2 + at.ox, :, :, high], rxb.at[zz], s_xb.at[zz], g_xb.at[zz], at.to_x())

    def xa(zz):
        return remote(a2a.at[zz * 2 + at.ox], rxa.at[zz], s_xa.at[zz], g_xa.at[zz], at.to_x())

    def yb(zz, j):
        yy = at.yat(j)
        return remote(a2b.at[zz, yy], ryb.at[at.y, zz], s_yb.at[zz, j], g_yb.at[at.y, zz], at.to_y(yy))

    def yb_in(zz, yy):
        return remote(ryb.at[yy, zz], ryb.at[yy, zz], s_yb.at[zz, 0], g_yb.at[yy, zz], at.to_x())

    def zc(k):
        zz = at.zat(k)
        return remote(a3.at[zz], rz.at[at.z], s_z.at[k], g_z.at[at.z], at.to_z(zz))

    def z_in(zz):
        return remote(rz.at[zz], rz.at[zz], s_z.at[0], g_z.at[zz], at.to_x())

    def each(k):
        return at.zat(k + 1)

    def begin(k):
        height = act_ref.shape[0] // depth
        made = jnp.dot(
            act_ref[pl.ds(pl.multiple_of(each(k) * height, height), height), :],
            dec_ref[...],
            preferred_element_type=F32,
        )
        part[pl.ds(each(k) * 2, 2)] = made.reshape((2,) + part.shape[1:]).astype(BF16)
        c_copy(each(k) * 2 + at.ox).start()
        c_copy(each(k) * 2 + at.x).start()

    def one(k):
        zz = each(k)
        for xx in (at.ox, at.x):
            d = zz * 2 + xx
            c_copy(d).wait_recv()
            a1[d] = (part[d, :, at.c].astype(F32) + rc[d].astype(F32)).astype(BF16)
            if xx is at.ox:
                xb(zz).start()
            for j in range(1, width):
                ya(d, j).start()

    def two(k):
        zz = each(k)
        for xx in (at.ox, at.x):
            d = zz * 2 + xx
            total = a1[d, at.y, :, low].astype(F32)
            for j in range(1, width):
                ya_in(d, at.yat(j)).wait_recv()
                total = total + rya[at.yat(j), d].astype(F32)
            a2a[d] = total.astype(BF16)
            if xx is at.ox:
                xa(zz).start()
        xb(zz).wait_recv()
        a2b[zz] = (a1[zz * 2 + at.x, :, :, high].astype(F32) + rxb[zz].astype(F32)).astype(BF16)
        for j in range(1, width):
            yb(zz, j).start()

    def sum_a(zz):
        xa(zz).wait_recv()
        return a2a[zz * 2 + at.x].astype(F32) + rxa[zz].astype(F32)

    def sum_b(zz):
        total = a2b[zz, at.y].astype(F32)
        for j in range(1, width):
            yb_in(zz, at.yat(j)).wait_recv()
            total = total + ryb[at.yat(j), zz].astype(F32)
        return total

    def three(k):
        zz = each(k)
        a3[zz, :, low] = sum_a(zz).astype(BF16)
        a3[zz, :, high] = sum_b(zz).astype(BF16)
        zc(k + 1).start()

    begin(0)
    begin(1)
    one(0)
    begin(2)
    one(1)
    two(0)

    def pipeline(k):
        begin(k)
        one(k - 1)
        two(k - 2)
        three(k - 3)

    loop(3, depth, pipeline)
    one(depth - 1)
    two(depth - 2)
    three(depth - 3)
    two(depth - 1)
    three(depth - 2)
    own = jnp.concatenate([sum_a(at.z), sum_b(at.z)], axis=-1)
    for k in range(1, depth):
        zz = at.zat(k)
        z_in(zz).wait_recv()
        own = own + rz[zz].astype(F32)
    residual = own + bias_ref[...] - tok_ref[at.y, at.c].astype(F32)
    scaled = residual * 0.25
    buf[at.dp, at.y, at.c] = scaled.astype(BF16)
    tz[at.z, 0:1, :] = jnp.sum(scaled, axis=0, keepdims=True)
    tz[at.z, 1:2, :] = jnp.sum(residual * residual, axis=0, keepdims=True)

    def tz_copy(k):
        return remote(tz.at[at.z], tz.at[at.z], s_tz.at[k], g_tz.at[at.z], at.to_z(at.zat(k)))

    def tz_in(zz):
        return remote(tz.at[zz], tz.at[zz], s_tz.at[0], g_tz.at[zz], at.to_x())

    for k in range(1, depth):
        tz_copy(k).start()
    x_stat = remote(tx.at[at.x], tx.at[at.x], s_tx, g_tx, at.to_x())
    c_stat = remote(tc.at[at.c], tc.at[at.c], s_tc, g_tc, at.to_c())

    def ty_copy(j):
        return remote(ty.at[at.y], ty.at[at.y], s_ty.at[j], g_ty.at[at.y], at.to_y(at.yat(j)))

    def stat_x():
        for k in range(1, depth):
            tz_in(at.zat(k)).wait_recv()
        tx[at.x] = jnp.sum(tz[...], axis=0)
        x_stat.start()

    def stat_y():
        x_stat.wait_recv()
        ty[at.y] = tx[0] + tx[1]
        for j in range(1, width):
            ty_copy(j).start()

    def stat_c():
        for j in range(1, width):
            yy = at.yat(j)
            remote(ty.at[yy], ty.at[yy], s_ty.at[0], g_ty.at[yy], at.to_x()).wait_recv()
        tc[at.c] = jnp.sum(ty[...], axis=0)
        c_stat.start()

    gather(at, buf, sems, (stat_x, stat_y, stat_c))
    c_stat.wait_recv()
    stat_ref[...] = tc[0] + tc[1]

    x_stat.wait_send()
    c_stat.wait_send()
    for j in range(1, width):
        ty_copy(j).wait_send()
    for k in range(1, depth):
        tz_copy(k).wait_send()
        zc(k).wait_send()

    def settle(k):
        zz = each(k)
        for xx in (at.ox, at.x):
            d = zz * 2 + xx
            c_copy(d).wait_send()
            for j in range(1, width):
                ya(d, j).wait_send()
        xb(zz).wait_send()
        xa(zz).wait_send()
        for j in range(1, width):
            yb(zz, j).wait_send()

    loop(0, depth, settle)


def reduce_gather(active, dec_weight, tokens, dec_bias, depth, width):
    feats = tokens.shape[1]
    rows = tokens.shape[0] // (width * 2)
    dps, half = depth * 2, feats // 2
    whole = active.shape[0] * feats * 2
    vmem = pl.BlockSpec(memory_space=pltpu.VMEM)
    block = pltpu.VMEM
    scratch = [
        block((dps, width, 2, rows, feats), BF16),
        block((dps, width, rows, feats), BF16),
        block((dps, width, rows, feats), BF16),
        block((width, dps, rows, half), BF16),
        block((dps, rows, half), BF16),
        block((depth, rows, half), BF16),
        block((depth, width, rows, half), BF16),
        block((depth, width, rows, half), BF16),
        block((width, depth, rows, half), BF16),
        block((depth, rows, feats), BF16),
        block((depth, rows, feats), BF16),
        block((depth, 2, feats), F32),
        block((2, 2, feats), F32),
        block((width, 2, feats), F32),
        block((2, 2, feats), F32),
        DMA((dps,)), DMA((dps,)),
        DMA((dps, width)), DMA((width, dps)),
        DMA((depth,)), DMA((depth,)),
        DMA((depth,)), DMA((depth,)),
        DMA((depth, width)), DMA((width, depth)),
        DMA((depth,)), DMA((depth,)),
        DMA((depth,)), DMA((depth,)),
        DMA, DMA,
        DMA((width,)), DMA((width,)),
        DMA, DMA,
    ] + gather_sems(depth, width)
    grads, stats = pl.pallas_call(
        functools.partial(reduce_kernel, depth, width),
        out_shape=(
            jax.ShapeDtypeStruct((dps, width, 2, rows, feats), BF16),
            jax.ShapeDtypeStruct((2, feats), F32),
        ),
        in_specs=[vmem] * 4,
        out_specs=(vmem, vmem),
        scratch_shapes=scratch,
        compiler_params=pltpu.CompilerParams(
            collective_id=1, has_side_effects=True, vmem_limit_bytes=7 * whole + 2 ** 22
        ),
        name="reduce_gather",
    )(
        active,
        dec_weight,
        tokens.reshape(width, 2, rows, feats),
        dec_bias.reshape(1, feats),
    )
    return grads.reshape(-1, feats), stats


def backward_kernel(tok_ref, act_ref, grad_ref, dec_ref, live_ref, enc_out, dec_out, bias_out, flipped):
    @pl.when(pl.program_id(0) == 0)
    def _():
        flipped[...] = tok_ref[...].T

    pre = lax.dot_general(grad_ref[...], dec_ref[...], (((1,), (1,)), ((), ())), preferred_element_type=F32)
    pieces = [
        jnp.where(live_ref[t : t + 1, :] > 0, pre[t * BLK : (t + 1) * BLK], 0.0) for t in range(live_ref.shape[0])
    ]
    pre = jnp.concatenate(pieces, axis=0)
    bias_out[...] = jnp.sum(pre, axis=0, keepdims=True)
    enc_out[...] = jnp.dot(flipped[...], pre.astype(BF16), preferred_element_type=F32).astype(BF16)
    dec_out[...] = lax.dot_general(
        act_ref[...], grad_ref[...], (((0,), (0,)), ((), ())), preferred_element_type=F32
    ).astype(BF16)


def backward(gathered, active, grads, dec_weight, live):
    rows, feats = gathered.shape
    latents = dec_weight.shape[0]
    tile = 2 * BLK
    live_cols = jnp.repeat(live.astype(F32), BLK, axis=1)
    vmem = pl.BlockSpec(memory_space=pltpu.VMEM)
    return pl.pallas_call(
        backward_kernel,
        grid=(latents // tile,),
        out_shape=(
            jax.ShapeDtypeStruct((feats, latents), BF16),
            jax.ShapeDtypeStruct((latents, feats), BF16),
            jax.ShapeDtypeStruct((1, latents), F32),
        ),
        in_specs=[
            vmem,
            pl.BlockSpec((rows, tile), lambda i: (0, i)),
            vmem,
            pl.BlockSpec((tile, feats), lambda i: (i, 0)),
            pl.BlockSpec((live.shape[0], tile), lambda i: (0, i)),
        ],
        out_specs=(
            pl.BlockSpec((feats, tile), lambda i: (0, i)),
            pl.BlockSpec((tile, feats), lambda i: (i, 0)),
            pl.BlockSpec((1, tile), lambda i: (0, i)),
        ),
        scratch_shapes=[pltpu.VMEM((feats, rows), BF16)],
        compiler_params=pltpu.CompilerParams(vmem_limit_bytes=10 * rows * feats),
        name="backward",
    )(gathered, active, grads, dec_weight, live_cols)


def local(depth, width, tokens, enc_weight, enc_bias, dec_weight, dec_bias, slot_token, slot_latent, slot_count):
    feats = tokens.shape[1]
    latents = enc_weight.shape[1]
    total_rows = tokens.shape[0] * depth * 2
    t_blocks, l_blocks = total_rows // BLK, latents // BLK
    alive = jnp.arange(slot_token.shape[0], dtype=jnp.int32) < slot_count[0]
    at_token = (slot_token[:, None] == jnp.arange(t_blocks, dtype=jnp.int32)[None, :]) & alive[:, None]
    at_latent = slot_latent[:, None] == jnp.arange(l_blocks, dtype=jnp.int32)[None, :]
    live = jnp.any(at_token[:, :, None] & at_latent[:, None, :], axis=0)
    mask = jnp.broadcast_to(live[:, None, :, None], (t_blocks, BLK, l_blocks, BLK)).reshape(total_rows, latents)

    gathered = gather_tokens(tokens, depth, width)
    dense = jnp.dot(gathered, enc_weight, preferred_element_type=F32) + enc_bias[None, :]
    active = jnp.where(mask, dense, 0.0).astype(BF16)
    grads, stats = reduce_gather(active, dec_weight, tokens, dec_bias, depth, width)
    enc_grad, dec_grad, bias_grad = backward(gathered, active, grads, dec_weight, live)
    return enc_grad, dec_grad, bias_grad.reshape(latents), stats[0], jnp.sum(stats[1]) / (total_rows * feats)


def solution(mesh):
    depth, width = mesh.shape["dp"] // 2, mesh.shape["latent"] // 2
    in_specs = (
        P("dp", None),
        P(None, ("dp", "latent")),
        P(("dp", "latent")),
        P(("dp", "latent"), None),
        P(),
        P(("dp", "latent")),
        P(("dp", "latent")),
        P(("dp", "latent")),
    )
    out_specs = (
        P(None, ("dp", "latent")),
        P(("dp", "latent"), None),
        P(("dp", "latent")),
        P(),
        P(),
    )
    return jax.shard_map(
        functools.partial(local, depth, width), mesh=mesh, in_specs=in_specs, out_specs=out_specs, check_vma=False
    )
```
